32 devices in a mesh: dp: 4 (over z), vocab: 8 (over y, x, core).
Axes of the slice: x: 2, y: 2, z: 4, core: 2. Of those that a mesh axis runs over, the one named last changes fastest.
Arguments:
- hidden: bfloat16 [2048, 5120], P('dp', 'vocab')
- weight: bfloat16 [5120, 19456], P(None, 'vocab'), may hold values from -0.078125 to 0.078125
- targets: int32 [2048], P('dp'), may hold values from 0 to 19455
- old_logprob: float32 [2048], P('dp'), may hold values from -13 to -10.5
- ref_logprob: float32 [2048], P('dp'), may hold values from -13 to -10.5
- lengths: int32 [32], P('dp'), may hold values from 1 to 64
- rewards: int32 [32], P('dp'), may hold values from 0 to 4
- group_ids: int32 [32], P('dp'), may hold values from 0 to 3, as said below
Outputs:
- token_logprob: float32 [2048], P('dp')
- entropy: float32 [2048], P('dp')
- advantage: float32 [2048], P('dp')
- loss: float32 [], replicated
The draws below stay inside these ranges and needn't reach their ends.
Inputs may be any that keep to these rules, and one draw needn't show every extreme that they name: `group_ids`: each prompt number is named by exactly 8 rollouts.
All inputs are finite; a program needn't handle non-finite values.
Results may differ from the reference program's by a relative error of at most 0.0003.
Values may be sent and summed in bfloat16 or wider, within the bound.
A program may use at most 128 MiB of HBM per device.

```python
import math
from functools import partial
import jax
import jax.numpy as jnp
import numpy as np
from jax import lax

D = 5120
SEQ = 64
GROUP = 8
VOCAB = 19456
TOK_DEV = 512
ROLLOUTS = 32
TOKENS = 2048
PROMPTS = 4


def draw_hidden(key, part):
    values = jax.random.normal(jax.random.fold_in(key, 11), (TOKENS, D), jnp.float32)
    return values.astype(jnp.bfloat16)


def draw_group_ids(key, part):
    order = jax.random.permutation(jax.random.fold_in(key, 21), ROLLOUTS)
    return (order // GROUP).astype(jnp.int32)


def plant(entries, key, smallest, largest):
    longest = entries.shape.index(max(entries.shape))
    spots = []
    for shift in (0, 1):
        where = [jax.random.randint(jax.random.fold_in(key, axis), (), 0, length) for axis, length in enumerate(entries.shape)]
        where[longest] = (where[longest] + shift) % entries.shape[longest]
        spots.append(tuple(where))
    return entries.at[spots[0]].set(smallest).at[spots[1]].set(largest)


def shard_levels(key, shape, shards, smallest, largest):
    loudness = 1.0
    for dim, blocks in shards:
        draws = jax.random.uniform(jax.random.fold_in(jax.random.fold_in(key, 6), dim), (blocks,), jnp.float32, smallest / len(shards), largest / len(shards))
        loudness = loudness * jnp.repeat(jnp.exp(draws), shape[dim] // blocks).reshape((-1,) + (1,) * (len(shape) - 1 - dim))
    return loudness


def cumulative_ranks(number_of, skew):
    weights = [(1 << 20) // math.isqrt(grade ** skew) + 1 for grade in range(1, number_of + 1)]
    scale = 1 + sum(weights) // (1 << 30)
    return np.cumsum(np.array([max(1, weight // scale) for weight in weights]))


def ranked_ids(key, dims, number_of, lean):
    grid = cumulative_ranks(number_of, lean)
    lot = jax.random.randint(jax.random.fold_in(key, 1), dims, 0, int(grid[number_of - 1]))
    grade = jnp.searchsorted(jnp.asarray(grid, jnp.int32), lot, side="right")
    return jax.random.permutation(jax.random.fold_in(key, 2), number_of)[grade].astype(jnp.int32)


def gaussian(own_key, shape, width, limit, pieces=(), kind=jnp.bfloat16):
    drawn = jax.random.normal(own_key, shape, jnp.float32) * width
    if len(pieces) > 0:
        drawn = shard_levels(own_key, shape, pieces, -0.22, 0.18) * drawn
    return jnp.clip(drawn, min=-limit, max=limit).astype(kind)


def setup_inputs(seed: int = 0) -> dict:
    streams_of = jax.random.split(jax.random.key(seed), 9)
    hidden = draw_hidden(jax.random.fold_in(streams_of[8], 71), 0)
    weight = gaussian(streams_of[1], (D, VOCAB), D ** -0.5, 0.078125, ((1, 8),))
    targets = plant(ranked_ids(streams_of[2], (TOKENS,), VOCAB, 2), jax.random.fold_in(streams_of[2], 3), 0, VOCAB - 1).astype(jnp.int32)
    old_logprob = jnp.clip(-13.0 + 2.5 * jax.random.uniform(streams_of[3], (TOKENS,), jnp.float32) ** shard_levels(streams_of[3], (TOKENS,), ((0, 4),), -0.2, 0.2), -13.0, -10.5)
    ref_logprob = jnp.clip(-13.0 + 2.5 * jax.random.uniform(streams_of[4], (TOKENS,), jnp.float32) ** shard_levels(streams_of[4], (TOKENS,), ((0, 4),), -0.2, 0.2), -13.0, -10.5)
    lengths = plant(jax.random.randint(streams_of[5], (ROLLOUTS,), 1, SEQ + 1), jax.random.fold_in(streams_of[5], 1), 1, SEQ).astype(jnp.int32)
    rewards = plant(jax.random.randint(streams_of[6], (ROLLOUTS,), 0, 5), jax.random.fold_in(streams_of[6], 1), 0, 4).astype(jnp.int32)
    group_ids = draw_group_ids(jax.random.fold_in(streams_of[8], 71), 0)
    return {"hidden": hidden, "weight": weight, "targets": targets, "old_logprob": old_logprob, "ref_logprob": ref_logprob, "lengths": lengths, "rewards": rewards, "group_ids": group_ids}


def head_block(weight, args):
    rows, picks = args
    logits = jnp.dot(rows, weight, preferred_element_type=jnp.float32)
    top = lax.optimization_barrier(jnp.max(logits, axis=1))
    scaled = jnp.exp(logits - top[:, None])
    total = lax.optimization_barrier(jnp.sum(scaled, axis=1))
    moment = lax.optimization_barrier(jnp.sum(scaled * logits, axis=1))
    lse = top + jnp.log(total)
    picked = jnp.take_along_axis(logits, picks[:, None], axis=1)[:, 0]
    return (picked - lse, lse - moment / total)

def reference(hidden, weight, targets, old_logprob, ref_logprob, lengths, rewards, group_ids):
    blocks = hidden.reshape(TOKENS // TOK_DEV, TOK_DEV, D)
    picks = targets.reshape(TOKENS // TOK_DEV, TOK_DEV).astype(jnp.int32)
    token_logprob, entropy = lax.map(partial(head_block, weight), (blocks, picks))
    token_logprob = token_logprob.reshape(TOKENS)
    entropy = entropy.reshape(TOKENS)
    member = (group_ids[:, None] == jnp.arange(PROMPTS, dtype=jnp.int32)[None, :]).astype(jnp.float32)
    scores = rewards.astype(jnp.float32)
    sums = jnp.dot(scores, member, precision=lax.Precision.HIGHEST)
    squares = jnp.dot(scores * scores, member, precision=lax.Precision.HIGHEST)
    mean = sums / GROUP
    spread = jnp.sqrt(jnp.maximum(squares / GROUP - mean * mean, 0.0))
    mean_r = jnp.dot(member, mean, precision=lax.Precision.HIGHEST)
    spread_r = jnp.dot(member, spread, precision=lax.Precision.HIGHEST)
    advantage = jnp.repeat((scores - mean_r) / jnp.maximum(spread_r, 1.0), SEQ)
    position = jnp.arange(SEQ, dtype=jnp.int32)
    mask = (position[None, :] < lengths[:, None]).astype(jnp.float32).reshape(TOKENS)
    ratio = jnp.exp(jnp.clip(token_logprob - old_logprob, -20.0, 20.0))
    surrogate = -jnp.minimum(ratio * advantage, jnp.clip(ratio, 0.8, 1.2) * advantage)
    shift = jnp.clip(ref_logprob - token_logprob, -20.0, 20.0)
    divergence = jnp.exp(shift) - shift - 1.0
    numer = jnp.sum(mask * (surrogate + 0.04 * divergence - 0.01 * entropy))
    loss = numer / jnp.sum(mask)
    return (token_logprob, entropy, advantage, loss)
```

```python
import functools

import jax
import jax.numpy as jnp
from jax import lax
from jax.experimental import pallas as pl
from jax.experimental.pallas import tpu as pltpu
from jax.sharding import PartitionSpec as P

GROUP = 8
LANES = 128
CHUNKS = 4
TILE = 512
MESH = pl.DeviceIdType.MESH


def kernel(n, dpn, h, w, tg, olp, rlp, lens, rew, gid, tok, ent, adv, loss,
           feats, wv, acc, tcol, part, st, dpa, dpb,
           hsem, wsem, ssem, rsem, st_s, st_r, dpa_s, dpa_r, dpb_s, dpb_r):
    me = lax.axis_index("vocab")
    my = lax.axis_index("dp")
    tokens, kdim = h.shape
    width = w.shape[1]
    nq = tokens // LANES
    nr = lens.shape[0]
    seq = tokens // nr
    grid = n == 8
    rows = tokens // CHUNKS

    if grid:
        core, cx, cy = me % 2, (me // 2) % 2, me // 4
        flip = 1 - 2 * core
        xn = (cy * 2 + (1 - cx)) * 2 + core
        yn = ((1 - cy) * 2 + cx) * 2 + core
        dn = ((1 - cy) * 2 + (1 - cx)) * 2 + core
        sib = me + flip
        owners = [me, sib, xn, xn + flip, yn, yn + flip, dn, dn + flip]

    def wcopy(slot, owner):
        return pltpu.make_async_copy(
            w.at[pl.ds(pl.multiple_of(owner * kdim, kdim), kdim), :], wv.at[slot], wsem.at[slot])

    def remote(src, dst, s, r, dev):
        return pltpu.make_async_remote_copy(
            src_ref=src, dst_ref=dst, send_sem=s, recv_sem=r,
            device_id=(my, dev), device_id_type=MESH)

    def todp(buf, s, r, dev):
        return pltpu.make_async_remote_copy(
            src_ref=buf.at[my], dst_ref=buf.at[my], send_sem=s.at[dev], recv_sem=r.at[my],
            device_id=(dev, me), device_id_type=MESH)

    hcopy = pltpu.make_async_copy(h, feats.at[0], hsem)
    hcopy.start()
    if grid:
        for s in range(n):
            wcopy(s, owners[s]).start()
    else:
        def wstart(s, c):
            wcopy(s, lax.rem(me - s + n, n)).start()
            return c
        lax.fori_loop(0, n, wstart, 0)

    barrier = pltpu.get_barrier_semaphore()
    for s in range(1, n):
        pl.semaphore_signal(barrier, inc=1, device_id=(my, lax.rem(me + s, n)), device_id_type=MESH)
    for s in range(1, dpn):
        pl.semaphore_signal(barrier, inc=1, device_id=(lax.rem(my + s, dpn), me), device_id_type=MESH)
    pl.semaphore_wait(barrier, n - 1 + dpn - 1)

    def span(r):
        return pl.ds(pl.multiple_of(r * rows, rows), rows)

    def half(r, i):
        return pl.ds(pl.multiple_of(r * rows + i * (rows // 2), rows // 2), rows // 2)

    def to_x(r):
        return remote(h.at[span(r)], feats.at[2, span(r)], ssem.at[2, r, 0], rsem.at[2, r, 0], xn)

    def to_y(r):
        return remote(h.at[span(r)], feats.at[4, span(r)], ssem.at[4, r, 0], rsem.at[4, r, 0], yn)

    def to_sib(slot, r):
        return remote(feats.at[slot, span(r)], feats.at[slot + 1, span(r)],
                      ssem.at[slot + 1, r, 0], rsem.at[slot + 1, r, 0], sib)

    def own_sib():
        return remote(h, feats.at[1], ssem.at[1, 0, 0], rsem.at[1, 0, 0], sib)

    def relay_y(r):
        return remote(feats.at[2, half(r, 0)], feats.at[6, half(r, 0)],
                      ssem.at[6, r, 0], rsem.at[6, r, 0], yn)

    def relay_x(r):
        return remote(feats.at[4, half(r, 1)], feats.at[6, half(r, 1)],
                      ssem.at[6, r, 1], rsem.at[6, r, 1], xn)

    def direct(s):
        return remote(h, feats.at[s], ssem.at[s, 0, 0], rsem.at[s, 0, 0], lax.rem(me + s, n))

    if grid:
        own_sib().start()
        for r in range(CHUNKS):
            to_x(r).start()
            to_y(r).start()
    else:
        def dstart(s, c):
            direct(s).start()
            return c
        lax.fori_loop(1, n, dstart, 0)

    lane = lax.broadcasted_iota(jnp.int32, (1, LANES), 1)
    sums = jnp.zeros((1, LANES), jnp.float32)
    squares = jnp.zeros((1, LANES), jnp.float32)
    total_len = 0
    for i in range(nr):
        score = rew[i].astype(jnp.float32)
        hit = lane == gid[i]
        sums = sums + jnp.where(hit, score, 0.0)
        squares = squares + jnp.where(hit, score * score, 0.0)
        total_len = total_len + jnp.clip(lens[i], 0, seq)
    count = jnp.zeros((1, LANES), jnp.float32) + total_len.astype(jnp.float32)
    dpa[my] = jnp.concatenate(
        [sums, squares, count, jnp.zeros((5, LANES), jnp.float32)], axis=0)

    lane_sq = lax.broadcasted_iota(jnp.int32, (LANES, LANES), 1)
    for q in range(nq):
        ids = jnp.broadcast_to(tg[q:q + 1, :] - me * width, (LANES, LANES))
        tcol[q * LANES:(q + 1) * LANES, :] = jnp.transpose(ids) - lane_sq

    for s in range(1, dpn):
        todp(dpa, dpa_s, dpa_r, lax.rem(my + s, dpn)).start()

    def mm(at, size, slots, first):
        for n0 in range(0, width, TILE):
            n1 = min(width, n0 + TILE)
            v = None if first else acc[pl.ds(at, size), n0:n1]
            for s in slots:
                d = jnp.dot(feats[s, pl.ds(at, size), :], wv[s, :, n0:n1],
                            preferred_element_type=jnp.float32)
                v = d if v is None else v + d
            acc[pl.ds(at, size), n0:n1] = v

    step = 16

    def stats_block(b, c):
        at = pl.multiple_of(b * step, step)
        cols = [acc[pl.ds(at, step), j:j + LANES] for j in range(0, width, LANES)]
        top = functools.reduce(jnp.maximum, cols)
        want = tcol[pl.ds(at, step), :]
        total = moment = pick = jnp.zeros((step, LANES), jnp.float32)
        for j, v in enumerate(cols):
            e = jnp.exp(v - top)
            total = total + e
            moment = moment + e * v
            pick = jnp.where(want == j * LANES, v, pick)
        part[0, pl.ds(at, step), :] = top
        part[1, pl.ds(at, step), :] = total
        part[2, pl.ds(at, step), :] = moment
        part[3, pl.ds(at, step), :] = pick
        return c

    def stats_rows(q):
        at = pl.multiple_of(q * LANES, LANES)
        lax.fori_loop(q * (LANES // step), (q + 1) * (LANES // step), stats_block, 0)
        m, t, mo, pk = (jnp.transpose(part[i, pl.ds(at, LANES), :]) for i in range(4))
        top = jnp.max(m, axis=0, keepdims=True)
        scale = jnp.exp(m - top)
        st[me, q] = jnp.concatenate(
            [top, jnp.sum(t * scale, axis=0, keepdims=True),
             jnp.sum(mo * scale, axis=0, keepdims=True), jnp.sum(pk, axis=0, keepdims=True),
             jnp.zeros((4, LANES), jnp.float32)], axis=0)

    hcopy.wait()
    if grid:
        wcopy(0, owners[0]).wait()
        own_sib().wait_recv()
        wcopy(1, owners[1]).wait()

        def own(r, c):
            mm(pl.multiple_of(r * rows, rows), rows, (0, 1), True)
            return c
        lax.fori_loop(0, CHUNKS, own, 0)
        for s in (2, 4, 3, 5):
            wcopy(s, owners[s]).wait()

        def sides(r, c):
            at = pl.multiple_of(r * rows, rows)
            to_x(r).wait_recv()
            to_y(r).wait_recv()
            relay_y(r).start()
            relay_x(r).start()
            to_sib(2, r).start()
            to_sib(4, r).start()
            mm(at, rows, (2, 4), False)
            to_sib(2, r).wait_recv()
            to_sib(4, r).wait_recv()
            mm(at, rows, (3, 5), False)
            return c
        lax.fori_loop(0, CHUNKS, sides, 0)
        for s in (6, 7):
            wcopy(s, owners[s]).wait()

        def corner(r, c):
            at = pl.multiple_of(r * rows, rows)
            relay_y(r).wait_recv()
            relay_x(r).wait_recv()
            to_sib(6, r).start()
            mm(at, rows, (6,), False)
            to_sib(6, r).wait_recv()
            mm(at, rows, (7,), False)
            for q in range(rows // LANES):
                stats_rows(r * (rows // LANES) + q)
            return c
        lax.fori_loop(0, CHUNKS, corner, 0)
    else:
        wcopy(0, me).wait()

        def first(r, c):
            mm(pl.multiple_of(r * rows, rows), rows, (0,), True)
            return c
        lax.fori_loop(0, CHUNKS, first, 0)

        def others(s, c):
            wcopy(s, lax.rem(me - s + n, n)).wait()
            direct(s).wait_recv()

            def inner(r, c2):
                mm(pl.multiple_of(r * rows, rows), rows, (s,), False)
                return c2
            lax.fori_loop(0, CHUNKS, inner, 0)
            return c
        lax.fori_loop(1, n, others, 0)

        def every(q, c):
            stats_rows(q)
            return c
        lax.fori_loop(0, nq, every, 0)

    def share(s):
        dev = lax.rem(me + s, n)
        return remote(st.at[me], st.at[me], st_s.at[s], st_r.at[me], dev)

    def shared(s):
        src = lax.rem(me + s, n)
        return remote(st.at[src], st.at[src], st_s.at[s], st_r.at[src], src)

    for s in range(1, n):
        share(s).start()

    for s in range(1, dpn):
        src = lax.rem(my + s, dpn)
        pltpu.make_async_remote_copy(
            src_ref=dpa.at[src], dst_ref=dpa.at[src], send_sem=dpa_s.at[src],
            recv_sem=dpa_r.at[src], device_id=(src, me), device_id_type=MESH).wait_recv()
    gathered = jnp.sum(dpa[...], axis=0)
    mean = gathered[0:1, :] / GROUP
    spread = jnp.sqrt(jnp.maximum(gathered[1:2, :] / GROUP - mean * mean, 0.0))
    count_all = gathered[2:3, :]
    roll = lax.broadcasted_iota(jnp.int32, (nr, LANES), 0)
    lanes = lax.broadcasted_iota(jnp.int32, (nr, LANES), 1)
    group = jnp.zeros((nr, LANES), jnp.int32)
    length = jnp.zeros((nr, LANES), jnp.int32)
    score = jnp.zeros((nr, LANES), jnp.float32)
    for i in range(nr):
        group = jnp.where(roll == i, gid[i], group)
        length = jnp.where(roll == i, lens[i], length)
        score = jnp.where(roll == i, rew[i].astype(jnp.float32), score)
    member = lanes == group
    mean_r = jnp.sum(jnp.where(member, mean, 0.0), axis=1, keepdims=True)
    spread_r = jnp.sum(jnp.where(member, spread, 0.0), axis=1, keepdims=True)
    adv_r = (score - mean_r) / jnp.maximum(spread_r, 1.0)
    advs, masks = [], []
    for q in range(nq):
        place = lanes + q * LANES - roll * seq
        inside = (place >= 0) & (place < seq)
        a = jnp.sum(jnp.where(inside, adv_r, 0.0), axis=0, keepdims=True)
        mk = jnp.sum(jnp.where(inside & (place < length), 1.0, 0.0), axis=0, keepdims=True)
        advs.append(a)
        masks.append(mk)
        adv[q:q + 1, :] = a

    for s in range(1, n):
        shared(s).wait_recv()
    numer = jnp.zeros((1, LANES), jnp.float32)
    for q in range(nq):
        a = st[:, q]
        top = jnp.max(a[:, 0:1, :], axis=0)
        scale = jnp.exp(a[:, 0:1, :] - top[None])
        total = jnp.sum(a[:, 1:2, :] * scale, axis=0)
        moment = jnp.sum(a[:, 2:3, :] * scale, axis=0)
        pick = jnp.sum(a[:, 3:4, :], axis=0)
        lse = top + jnp.log(total)
        lp = pick - lse
        en = lse - moment / total
        tok[q:q + 1, :] = lp
        ent[q:q + 1, :] = en
        ratio = jnp.exp(jnp.clip(lp - olp[q:q + 1, :], -20.0, 20.0))
        sur = -jnp.minimum(ratio * advs[q], jnp.clip(ratio, 0.8, 1.2) * advs[q])
        shift = jnp.clip(rlp[q:q + 1, :] - lp, -20.0, 20.0)
        div = jnp.exp(shift) - shift - 1.0
        numer = numer + masks[q] * (sur + 0.04 * div - 0.01 * en)
    dpb[my] = jnp.broadcast_to(numer, (8, LANES))
    for s in range(1, dpn):
        todp(dpb, dpb_s, dpb_r, lax.rem(my + s, dpn)).start()

    if grid:
        own_sib().wait_send()

        def drain(r, c):
            to_x(r).wait_send()
            to_y(r).wait_send()
            relay_y(r).wait_send()
            relay_x(r).wait_send()
            for s in (2, 4, 6):
                to_sib(s, r).wait_send()
            return c
        lax.fori_loop(0, CHUNKS, drain, 0)
    else:
        def ddrain(s, c):
            direct(s).wait_send()
            return c
        lax.fori_loop(1, n, ddrain, 0)
    for s in range(1, n):
        share(s).wait_send()
    for s in range(1, dpn):
        todp(dpa, dpa_s, dpa_r, lax.rem(my + s, dpn)).wait_send()
    for s in range(1, dpn):
        src = lax.rem(my + s, dpn)
        pltpu.make_async_remote_copy(
            src_ref=dpb.at[src], dst_ref=dpb.at[src], send_sem=dpb_s.at[src],
            recv_sem=dpb_r.at[src], device_id=(src, me), device_id_type=MESH).wait_recv()
    ratio = jnp.sum(dpb[:, 0:1, :], axis=0)
    loss[0] = jnp.sum(ratio) / jnp.max(count_all)
    for s in range(1, dpn):
        todp(dpb, dpb_s, dpb_r, lax.rem(my + s, dpn)).wait_send()


def per_device(n, dpn, hidden, weight, targets, old_logprob, ref_logprob, lengths, rewards, group_ids):
    tokens, kdim = hidden.shape
    width = weight.shape[1]
    nq = tokens // LANES
    anyspec = pl.BlockSpec(memory_space=pl.ANY)
    vmem = pl.BlockSpec(memory_space=pltpu.VMEM)
    smem = pl.BlockSpec(memory_space=pltpu.SMEM)
    dma = pltpu.SemaphoreType.DMA
    tile = jax.ShapeDtypeStruct((nq, LANES), jnp.float32)
    tok, ent, adv, loss = pl.pallas_call(
        functools.partial(kernel, n, dpn),
        out_shape=(tile, tile, tile, jax.ShapeDtypeStruct((1,), jnp.float32)),
        in_specs=[anyspec, anyspec, vmem, vmem, vmem, smem, smem, smem],
        out_specs=(vmem, vmem, vmem, smem),
        scratch_shapes=[
            pltpu.VMEM((n, tokens, kdim), jnp.bfloat16),
            pltpu.VMEM((n, kdim, width), jnp.bfloat16),
            pltpu.VMEM((tokens, width), jnp.float32),
            pltpu.VMEM((tokens, LANES), jnp.int32),
            pltpu.VMEM((4, tokens, LANES), jnp.float32),
            pltpu.VMEM((n, nq, 8, LANES), jnp.float32),
            pltpu.VMEM((dpn, 8, LANES), jnp.float32),
            pltpu.VMEM((dpn, 8, LANES), jnp.float32),
            dma, dma((n,)), dma((n, CHUNKS, 2)), dma((n, CHUNKS, 2)),
            dma((n,)), dma((n,)), dma((dpn,)), dma((dpn,)), dma((dpn,)), dma((dpn,)),
        ],
        compiler_params=pltpu.CompilerParams(
            collective_id=0, has_side_effects=True, vmem_limit_bytes=60 * 1024 * 1024),
        name="policy_loss",
    )(hidden, weight, targets.reshape(nq, LANES), old_logprob.reshape(nq, LANES),
      ref_logprob.reshape(nq, LANES), lengths, rewards, group_ids)
    return tok.reshape(tokens), ent.reshape(tokens), adv.reshape(tokens), loss.reshape(())


def solution(mesh):
    return jax.shard_map(
        functools.partial(per_device, mesh.shape["vocab"], mesh.shape["dp"]),
        mesh=mesh,
        in_specs=(
            P("dp", "vocab"),
            P(None, "vocab"),
            P("dp"),
            P("dp"),
            P("dp"),
            P("dp"),
            P("dp"),
            P("dp"),
        ),
        out_specs=(P("dp"), P("dp"), P("dp"), P()),
        check_vma=False,
    )
```

```python
import functools

import jax
import jax.numpy as jnp
from jax import lax
from jax.experimental import pallas as pl
from jax.experimental.pallas import tpu as pltpu
from jax.sharding import PartitionSpec as P

GROUP = 8
LANES = 128
CHUNKS = 2
TILE = 512
MESH = pl.DeviceIdType.MESH


def kernel(n, dpn, h, w, tg, olp, rlp, lens, rew, gid, res, loss,
           feats, wv, acc, tcol, part, st, dpa, dpb,
           hsem, wsem, ssem, rsem, st_s, st_r, dpa_s, dpa_r, dpb_s, dpb_r):
    me = lax.axis_index("vocab")
    my = lax.axis_index("dp")
    tokens, kdim = h.shape
    width = w.shape[1]
    nq = tokens // LANES
    nr = lens.shape[0]
    tok, ent, adv = res.at[0], res.at[1], res.at[2]
    seq = tokens // nr
    grid = n == 8
    rows = tokens // CHUNKS

    if grid:
        core, cx, cy = me % 2, (me // 2) % 2, me // 4
        flip = 1 - 2 * core
        xn = (cy * 2 + (1 - cx)) * 2 + core
        yn = ((1 - cy) * 2 + cx) * 2 + core
        dn = ((1 - cy) * 2 + (1 - cx)) * 2 + core
        sib = me + flip
        owners = [me, sib, xn, xn + flip, yn, yn + flip, dn, dn + flip]

    def wcopy(slot, owner):
        return pltpu.make_async_copy(
            w.at[pl.ds(pl.multiple_of(owner * kdim, kdim), kdim), :], wv.at[slot], wsem.at[slot])

    def remote(src, dst, s, r, dev):
        return pltpu.make_async_remote_copy(
            src_ref=src, dst_ref=dst, send_sem=s, recv_sem=r,
            device_id=(my, dev), device_id_type=MESH)

    def todp(buf, s, r, dev):
        return pltpu.make_async_remote_copy(
            src_ref=buf.at[my], dst_ref=buf.at[my], send_sem=s.at[dev], recv_sem=r.at[my],
            device_id=(dev, me), device_id_type=MESH)

    hcopy = pltpu.make_async_copy(h, feats.at[0], hsem)
    hcopy.start()
    if grid:
        for s in range(2):
            wcopy(s, owners[s]).start()
    else:
        def wstart(s, c):
            wcopy(s, lax.rem(me - s + n, n)).start()
            return c
        lax.fori_loop(0, n, wstart, 0)

    barrier = pltpu.get_barrier_semaphore()
    for s in range(1, n):
        pl.semaphore_signal(barrier, inc=1, device_id=(my, lax.rem(me + s, n)), device_id_type=MESH)
    for s in range(1, dpn):
        pl.semaphore_signal(barrier, inc=1, device_id=(lax.rem(my + s, dpn), me), device_id_type=MESH)
    pl.semaphore_wait(barrier, n - 1 + dpn - 1)

    def span(r):
        return pl.ds(pl.multiple_of(r * rows, rows), rows)

    def half(r, i):
        return pl.ds(pl.multiple_of(r * rows + i * (rows // 2), rows // 2), rows // 2)

    def to_x(r):
        return remote(h.at[span(r)], feats.at[2, span(r)], ssem.at[2, r, 0], rsem.at[2, r, 0], xn)

    def to_y(r):
        return remote(h.at[span(r)], feats.at[4, span(r)], ssem.at[4, r, 0], rsem.at[4, r, 0], yn)

    def to_sib(slot, r):
        return remote(feats.at[slot, span(r)], feats.at[slot + 1, span(r)],
                      ssem.at[slot + 1, r, 0], rsem.at[slot + 1, r, 0], sib)

    def own_sib():
        return remote(h, feats.at[1], ssem.at[1, 0, 0], rsem.at[1, 0, 0], sib)

    def relay_y(r):
        return remote(feats.at[2, half(r, 0)], feats.at[6, half(r, 0)],
                      ssem.at[6, r, 0], rsem.at[6, r, 0], yn)

    def relay_x(r):
        return remote(feats.at[4, half(r, 1)], feats.at[6, half(r, 1)],
                      ssem.at[6, r, 1], rsem.at[6, r, 1], xn)

    def direct(s):
        return remote(h, feats.at[s], ssem.at[s, 0, 0], rsem.at[s, 0, 0], lax.rem(me + s, n))

    if grid:
        own_sib().start()
        for r in range(CHUNKS):
            to_x(r).start()
            to_y(r).start()
    else:
        def dstart(s, c):
            direct(s).start()
            return c
        lax.fori_loop(1, n, dstart, 0)

    lane = lax.broadcasted_iota(jnp.int32, (1, LANES), 1)
    sums = jnp.zeros((1, LANES), jnp.float32)
    squares = jnp.zeros((1, LANES), jnp.float32)
    total_len = 0
    for i in range(nr):
        score = rew[i].astype(jnp.float32)
        hit = lane == gid[i]
        sums = sums + jnp.where(hit, score, 0.0)
        squares = squares + jnp.where(hit, score * score, 0.0)
        total_len = total_len + jnp.clip(lens[i], 0, seq)
    count = jnp.zeros((1, LANES), jnp.float32) + total_len.astype(jnp.float32)
    dpa[my] = jnp.concatenate(
        [sums, squares, count, jnp.zeros((5, LANES), jnp.float32)], axis=0)

    lane_sq = lax.broadcasted_iota(jnp.int32, (LANES, LANES), 1)
    for q in range(nq):
        ids = jnp.broadcast_to(tg[q:q + 1, :] - me * width, (LANES, LANES))
        tcol[q * LANES:(q + 1) * LANES, :] = jnp.transpose(ids) - lane_sq

    for s in range(1, dpn):
        todp(dpa, dpa_s, dpa_r, lax.rem(my + s, dpn)).start()

    def mm(at, size, slots, first):
        for n0 in range(0, width, TILE):
            n1 = min(width, n0 + TILE)
            v = None if first else acc[pl.ds(at, size), n0:n1]
            for s in slots:
                d = jnp.dot(feats[s, pl.ds(at, size), :], wv[s, :, n0:n1],
                            preferred_element_type=jnp.float32)
                v = d if v is None else v + d
            acc[pl.ds(at, size), n0:n1] = v

    step = 16

    def stats_block(b, c):
        at = pl.multiple_of(b * step, step)
        cols = [acc[pl.ds(at, step), j:j + LANES] for j in range(0, width, LANES)]
        top = functools.reduce(jnp.maximum, cols)
        want = tcol[pl.ds(at, step), :]
        total = moment = pick = jnp.zeros((step, LANES), jnp.float32)
        for j, v in enumerate(cols):
            e = jnp.exp(v - top)
            total = total + e
            moment = moment + e * v
            pick = jnp.where(want == j * LANES, v, pick)
        part[0, pl.ds(at, step), :] = top
        part[1, pl.ds(at, step), :] = total
        part[2, pl.ds(at, step), :] = moment
        part[3, pl.ds(at, step), :] = pick
        return c

    def stats_rows(q):
        at = pl.multiple_of(q * LANES, LANES)
        lax.fori_loop(q * (LANES // step), (q + 1) * (LANES // step), stats_block, 0)
        m, t, mo, pk = (jnp.transpose(part[i, pl.ds(at, LANES), :]) for i in range(4))
        top = jnp.max(m, axis=0, keepdims=True)
        scale = jnp.exp(m - top)
        st[me, q] = jnp.concatenate(
            [top, jnp.sum(t * scale, axis=0, keepdims=True),
             jnp.sum(mo * scale, axis=0, keepdims=True), jnp.sum(pk, axis=0, keepdims=True),
             jnp.zeros((4, LANES), jnp.float32)], axis=0)

    hcopy.wait()
    if grid:
        wcopy(0, owners[0]).wait()
        wcopy(2, owners[2]).start()

        def own(r, c):
            mm(pl.multiple_of(r * rows, rows), rows, (0,), True)
            return c
        lax.fori_loop(0, CHUNKS, own, 0)
        own_sib().wait_recv()
        wcopy(1, owners[1]).wait()
        wcopy(4, owners[4]).start()
        wcopy(3, owners[3]).start()

        def pair(r, c):
            mm(pl.multiple_of(r * rows, rows), rows, (1,), False)
            return c
        lax.fori_loop(0, CHUNKS, pair, 0)
        wcopy(2, owners[2]).wait()
        wcopy(5, owners[5]).start()
        wcopy(6, owners[6]).start()
        wcopy(4, owners[4]).wait()
        wcopy(7, owners[7]).start()
        for s in (3, 5):
            wcopy(s, owners[s]).wait()

        def sides(r, c):
            at = pl.multiple_of(r * rows, rows)
            to_x(r).wait_recv()
            to_y(r).wait_recv()
            relay_y(r).start()
            relay_x(r).start()
            to_sib(2, r).start()
            to_sib(4, r).start()
            mm(at, rows, (2, 4), False)
            to_sib(2, r).wait_recv()
            to_sib(4, r).wait_recv()
            mm(at, rows, (3, 5), False)
            return c
        lax.fori_loop(0, CHUNKS, sides, 0)
        for s in (6, 7):
            wcopy(s, owners[s]).wait()

        def corner(r, c):
            at = pl.multiple_of(r * rows, rows)
            relay_y(r).wait_recv()
            relay_x(r).wait_recv()
            to_sib(6, r).start()
            mm(at, rows, (6,), False)
            to_sib(6, r).wait_recv()
            mm(at, rows, (7,), False)
            for q in range(rows // LANES):
                stats_rows(r * (rows // LANES) + q)
            return c
        lax.fori_loop(0, CHUNKS, corner, 0)
    else:
        wcopy(0, me).wait()

        def first(r, c):
            mm(pl.multiple_of(r * rows, rows), rows, (0,), True)
            return c
        lax.fori_loop(0, CHUNKS, first, 0)

        def others(s, c):
            wcopy(s, lax.rem(me - s + n, n)).wait()
            direct(s).wait_recv()

            def inner(r, c2):
                mm(pl.multiple_of(r * rows, rows), rows, (s,), False)
                return c2
            lax.fori_loop(0, CHUNKS, inner, 0)
            return c
        lax.fori_loop(1, n, others, 0)

        def every(q, c):
            stats_rows(q)
            return c
        lax.fori_loop(0, nq, every, 0)

    def share(s):
        dev = lax.rem(me + s, n)
        return remote(st.at[me], st.at[me], st_s.at[s], st_r.at[me], dev)

    def shared(s):
        src = lax.rem(me + s, n)
        return remote(st.at[src], st.at[src], st_s.at[s], st_r.at[src], src)

    for s in range(1, n):
        share(s).start()

    for s in range(1, dpn):
        src = lax.rem(my + s, dpn)
        pltpu.make_async_remote_copy(
            src_ref=dpa.at[src], dst_ref=dpa.at[src], send_sem=dpa_s.at[src],
            recv_sem=dpa_r.at[src], device_id=(src, me), device_id_type=MESH).wait_recv()
    gathered = jnp.sum(dpa[...], axis=0)
    mean = gathered[0:1, :] / GROUP
    spread = jnp.sqrt(jnp.maximum(gathered[1:2, :] / GROUP - mean * mean, 0.0))
    count_all = gathered[2:3, :]
    roll = lax.broadcasted_iota(jnp.int32, (nr, LANES), 0)
    lanes = lax.broadcasted_iota(jnp.int32, (nr, LANES), 1)
    group = jnp.zeros((nr, LANES), jnp.int32)
    length = jnp.zeros((nr, LANES), jnp.int32)
    score = jnp.zeros((nr, LANES), jnp.float32)
    for i in range(nr):
        group = jnp.where(roll == i, gid[i], group)
        length = jnp.where(roll == i, lens[i], length)
        score = jnp.where(roll == i, rew[i].astype(jnp.float32), score)
    member = lanes == group
    mean_r = jnp.sum(jnp.where(member, mean, 0.0), axis=1, keepdims=True)
    spread_r = jnp.sum(jnp.where(member, spread, 0.0), axis=1, keepdims=True)
    adv_r = (score - mean_r) / jnp.maximum(spread_r, 1.0)
    advs, masks = [], []
    for q in range(nq):
        place = lanes + q * LANES - roll * seq
        inside = (place >= 0) & (place < seq)
        a = jnp.sum(jnp.where(inside, adv_r, 0.0), axis=0, keepdims=True)
        mk = jnp.sum(jnp.where(inside & (place < length), 1.0, 0.0), axis=0, keepdims=True)
        advs.append(a)
        masks.append(mk)
        adv[q:q + 1, :] = a

    for s in range(1, n):
        shared(s).wait_recv()
    numer = jnp.zeros((1, LANES), jnp.float32)
    for q in range(nq):
        a = st[:, q]
        top = jnp.max(a[:, 0:1, :], axis=0)
        scale = jnp.exp(a[:, 0:1, :] - top[None])
        total = jnp.sum(a[:, 1:2, :] * scale, axis=0)
        moment = jnp.sum(a[:, 2:3, :] * scale, axis=0)
        pick = jnp.sum(a[:, 3:4, :], axis=0)
        lse = top + jnp.log(total)
        lp = pick - lse
        en = lse - moment / total
        tok[q:q + 1, :] = lp
        ent[q:q + 1, :] = en
        ratio = jnp.exp(jnp.clip(lp - olp[q:q + 1, :], -20.0, 20.0))
        sur = -jnp.minimum(ratio * advs[q], jnp.clip(ratio, 0.8, 1.2) * advs[q])
        shift = jnp.clip(rlp[q:q + 1, :] - lp, -20.0, 20.0)
        div = jnp.exp(shift) - shift - 1.0
        numer = numer + masks[q] * (sur + 0.04 * div - 0.01 * en)
    dpb[my] = jnp.broadcast_to(numer, (8, LANES))
    for s in range(1, dpn):
        todp(dpb, dpb_s, dpb_r, lax.rem(my + s, dpn)).start()

    if grid:
        own_sib().wait_send()

        def drain(r, c):
            to_x(r).wait_send()
            to_y(r).wait_send()
            relay_y(r).wait_send()
            relay_x(r).wait_send()
            for s in (2, 4, 6):
                to_sib(s, r).wait_send()
            return c
        lax.fori_loop(0, CHUNKS, drain, 0)
    else:
        def ddrain(s, c):
            direct(s).wait_send()
            return c
        lax.fori_loop(1, n, ddrain, 0)
    for s in range(1, n):
        share(s).wait_send()
    for s in range(1, dpn):
        todp(dpa, dpa_s, dpa_r, lax.rem(my + s, dpn)).wait_send()
    for s in range(1, dpn):
        src = lax.rem(my + s, dpn)
        pltpu.make_async_remote_copy(
            src_ref=dpb.at[src], dst_ref=dpb.at[src], send_sem=dpb_s.at[src],
            recv_sem=dpb_r.at[src], device_id=(src, me), device_id_type=MESH).wait_recv()
    ratio = jnp.sum(dpb[:, 0:1, :], axis=0)
    loss[0] = jnp.sum(ratio) / jnp.max(count_all)
    for s in range(1, dpn):
        todp(dpb, dpb_s, dpb_r, lax.rem(my + s, dpn)).wait_send()


def per_device(n, dpn, hidden, weight, targets, old_logprob, ref_logprob, lengths, rewards, group_ids):
    tokens, kdim = hidden.shape
    width = weight.shape[1]
    nq = tokens // LANES
    anyspec = pl.BlockSpec(memory_space=pl.ANY)
    vmem = pl.BlockSpec(memory_space=pltpu.VMEM)
    smem = pl.BlockSpec(memory_space=pltpu.SMEM)
    dma = pltpu.SemaphoreType.DMA
    res, loss = pl.pallas_call(
        functools.partial(kernel, n, dpn),
        out_shape=(jax.ShapeDtypeStruct((3, nq, LANES), jnp.float32),
                   jax.ShapeDtypeStruct((1,), jnp.float32)),
        in_specs=[anyspec, anyspec, vmem, vmem, vmem, smem, smem, smem],
        out_specs=(vmem, smem),
        scratch_shapes=[
            pltpu.VMEM((n, tokens, kdim), jnp.bfloat16),
            pltpu.VMEM((n, kdim, width), jnp.bfloat16),
            pltpu.VMEM((tokens, width), jnp.float32),
            pltpu.VMEM((tokens, LANES), jnp.int32),
            pltpu.VMEM((4, tokens, LANES), jnp.float32),
            pltpu.VMEM((n, nq, 8, LANES), jnp.float32),
            pltpu.VMEM((dpn, 8, LANES), jnp.float32),
            pltpu.VMEM((dpn, 8, LANES), jnp.float32),
            dma, dma((n,)), dma((n, CHUNKS, 2)), dma((n, CHUNKS, 2)),
            dma((n,)), dma((n,)), dma((dpn,)), dma((dpn,)), dma((dpn,)), dma((dpn,)),
        ],
        compiler_params=pltpu.CompilerParams(
            collective_id=0, has_side_effects=True, vmem_limit_bytes=60 * 1024 * 1024),
        name="policy_loss",
    )(hidden, weight, targets.reshape(nq, LANES), old_logprob.reshape(nq, LANES),
      ref_logprob.reshape(nq, LANES), lengths, rewards, group_ids)
    return res[0].reshape(tokens), res[1].reshape(tokens), res[2].reshape(tokens), loss.reshape(())


def solution(mesh):
    return jax.shard_map(
        functools.partial(per_device, mesh.shape["vocab"], mesh.shape["dp"]),
        mesh=mesh,
        in_specs=(
            P("dp", "vocab"),
            P(None, "vocab"),
            P("dp"),
            P("dp"),
            P("dp"),
            P("dp"),
            P("dp"),
            P("dp"),
        ),
        out_specs=(P("dp"), P("dp"), P("dp"), P()),
        check_vma=False,
    )
```
